32 devices in a mesh: dp: 4 (over z), row: 2 (over y), col: 4 (over x, core).
Axes of the slice: x: 2, y: 2, z: 4, core: 2. Of those that a mesh axis runs over, the one named last changes fastest.
Arguments:
- hidden_in: bfloat16 [8, 512, 2048], P('dp', 'row', 'col'), may hold values from -6 to 6
- w_qkv: bfloat16 [2, 2048, 3, 2048], P(None, 'row', None, 'col'), as said below
- w_out: bfloat16 [2, 2048, 2048], P(None, 'row', 'col'), may hold values from -0.125 to 0.125
- w_gate_up: bfloat16 [2, 2048, 2, 8192], P(None, 'row', None, 'col'), may hold values from -0.125 to 0.125
- w_down: bfloat16 [2, 8192, 2048], P(None, 'row', 'col'), may hold values from -0.0625 to 0.0625
- norm_gains: float32 [2, 4, 2048], P(None, None, 'col'), as said below
- grad_out: bfloat16 [8, 512, 2048], P('dp', 'row', 'col'), may hold values from -6 to 6
Outputs:
- hidden_out: bfloat16 [8, 512, 2048], P('dp', 'row', 'col')
- grad_in: float32 [8, 512, 2048], P('dp', 'row', 'col')
- grad_qkv: float32 [2, 2048, 3, 2048], P(None, 'row', None, 'col')
- grad_wout: float32 [2, 2048, 2048], P(None, 'row', 'col')
- grad_gate_up: float32 [2, 2048, 2, 8192], P(None, 'row', None, 'col')
- grad_down: float32 [2, 8192, 2048], P(None, 'row', 'col')
- grad_gains: float32 [2, 4, 2048], P(None, None, 'col')
The draws below stay inside these ranges and needn't reach their ends.
Inputs may be any that keep to these rules, and one draw needn't show every extreme that they name: `w_qkv`: every entry's magnitude is at most 4 / sqrt(2048). `norm_gains`: every gain lies between 0.5 and 1.5.
All inputs are finite; a program needn't handle non-finite values.
Results may differ from the reference program's by a relative error of at most 0.04.
Values may be sent and summed in bfloat16 or wider, within the bound.
No kernel may reach another device: no remote copies, remote signals or barrier semaphores. Data moves between devices by JAX's collectives and lax.ppermute only.
A program may use at most 384 MiB of HBM per device.

```python
import jax
import jax.numpy as jnp
from jax import lax

D = 2048
H = 16
HD = 128
FF = 8192
LAYERS = 2
LEN = 512
SEQS = 8


def draw_w_qkv(key, part):
    deviation = D ** (-0.5)
    return (jax.random.truncated_normal(jax.random.fold_in(key, 1), -4.0, 4.0, (LAYERS, D, 3, D), jnp.float32) * deviation).astype(jnp.bfloat16)


def draw_norm_gains(key, part):
    gain_draw = jax.random.uniform(jax.random.fold_in(key, 5), (LAYERS, 4, D), jnp.float32, 0.5, 1.5)
    return gain_draw


def levels(own_key, extent, shards, smallest, high):
    level = 1.0
    for position, blocks in shards:
        heights = jax.random.uniform(jax.random.fold_in(jax.random.fold_in(own_key, 6), position), (blocks,), jnp.float32, smallest / len(shards), high / len(shards))
        level = level * jnp.repeat(jnp.exp(heights), extent[position] // blocks).reshape((-1,) + (1,) * (len(extent) - 1 - position))
    return level


def gaussian(key, extent, width, reach, shards=(), held_as=jnp.bfloat16):
    gain = levels(key, extent, shards, -0.22, 0.18) if shards else 1.0
    array = jax.random.normal(key, extent, jnp.float32) * width * gain
    return jnp.minimum(jnp.maximum(array, -reach), reach).astype(held_as)


def setup_inputs(seed: int = 0) -> dict:
    seeds = jax.random.split(jax.random.key(seed), 8)
    return {
        "hidden_in": gaussian(seeds[0], (SEQS, LEN, D), 1.0, 6.0, ((0, 4), (1, 2), (2, 4))),
        "w_qkv": draw_w_qkv(jax.random.fold_in(seeds[7], 71), 0),
        "w_out": gaussian(seeds[2], (LAYERS, D, D), D ** -0.5, 0.125, ((1, 2), (2, 4))),
        "w_gate_up": gaussian(seeds[3], (LAYERS, D, 2, FF), D ** -0.5, 0.125, ((1, 2), (3, 4))),
        "w_down": gaussian(seeds[4], (LAYERS, FF, D), FF ** -0.5, 0.0625, ((1, 2), (2, 4))),
        "norm_gains": draw_norm_gains(jax.random.fold_in(seeds[7], 71), 0),
        "grad_out": gaussian(seeds[6], (SEQS, LEN, D), 1.0, 6.0, ((0, 4), (1, 2), (2, 4))),
    }


EPS = 1e-06
NEG = -1e+30

def rms_parts(values):
    inverse = lax.rsqrt(lax.optimization_barrier(jnp.mean(values * values, axis=-1, keepdims=True)) + EPS)
    return (values * inverse, inverse)

def norm_back(upstream, normed, inverse):
    center = lax.optimization_barrier(jnp.mean(upstream * normed, axis=-1, keepdims=True))
    return inverse * (upstream - normed * center)

def causal_scores(query_bf, key_bf):
    length = query_bf.shape[0]
    query4 = query_bf.reshape(length, H, HD).astype(jnp.float32)
    key4 = key_bf.reshape(length, H, HD).astype(jnp.float32)
    scores = jnp.einsum('qhd,khd->hqk', query4, key4) * HD ** (-0.5)
    positions = jnp.arange(length)
    allowed = positions[None, :] <= positions[:, None]
    return jnp.where(allowed[None], scores, NEG)

def forward_layer(resid, wqkv, wout, wgu, wdown, gains):
    length = resid.shape[0]
    resid_bf = resid.astype(jnp.bfloat16)
    proj = jnp.dot(resid_bf, wqkv.reshape(D, 3 * D), preferred_element_type=jnp.float32).reshape(length, 3, D)
    query_n, query_inv = rms_parts(proj[:, 0])
    key_n, key_inv = rms_parts(proj[:, 1])
    query_bf = (query_n * gains[0]).astype(jnp.bfloat16)
    key_bf = (key_n * gains[1]).astype(jnp.bfloat16)
    value_bf = proj[:, 2].astype(jnp.bfloat16)
    scores = causal_scores(query_bf, key_bf)
    top = lax.optimization_barrier(jnp.max(scores, axis=-1, keepdims=True))
    expo = jnp.exp(scores - top)
    total = lax.optimization_barrier(jnp.sum(expo, axis=-1, keepdims=True))
    probs = expo / total
    logsum = top + jnp.log(total)
    value4 = value_bf.reshape(length, H, HD).astype(jnp.float32)
    attn = jnp.einsum('hqk,khd->qhd', probs.astype(jnp.bfloat16).astype(jnp.float32), value4)
    attn_bf = attn.reshape(length, D).astype(jnp.bfloat16)
    attn_proj = jnp.dot(attn_bf, wout, preferred_element_type=jnp.float32)
    attn_n, attn_inv = rms_parts(attn_proj)
    middle = resid + gains[2] * attn_n
    middle_bf = middle.astype(jnp.bfloat16)
    gate_up = jnp.dot(middle_bf, wgu.reshape(D, 2 * FF), preferred_element_type=jnp.float32).reshape(length, 2, FF)
    gate_pre, up_pre = (gate_up[:, 0], gate_up[:, 1])
    hidden_bf = (jax.nn.silu(gate_pre) * up_pre).astype(jnp.bfloat16)
    mlp_proj = jnp.dot(hidden_bf, wdown, preferred_element_type=jnp.float32)
    mlp_n, mlp_inv = rms_parts(mlp_proj)
    output = middle + gains[3] * mlp_n
    saved = (resid_bf, query_n, query_inv, key_n, key_inv, query_bf, key_bf, value_bf, logsum, attn_bf, attn_n, attn_inv, middle_bf, gate_pre, up_pre, hidden_bf, mlp_n, mlp_inv)
    return (output, saved)

def backward_layer(upstream, wqkv, wout, wgu, wdown, gains, saved):
    resid_bf, query_n, query_inv, key_n, key_inv, query_bf, key_bf, value_bf, logsum, attn_bf, attn_n, attn_inv, middle_bf, gate_pre, up_pre, hidden_bf, mlp_n, mlp_inv = saved
    length = upstream.shape[0]
    gain_mlp = lax.optimization_barrier(jnp.sum(upstream * mlp_n, axis=0))
    mlp_grad = norm_back(upstream * gains[3], mlp_n, mlp_inv).astype(jnp.bfloat16)
    down_grad = jnp.dot(hidden_bf.T, mlp_grad, preferred_element_type=jnp.float32)
    hidden_grad = jnp.dot(mlp_grad, wdown.T, preferred_element_type=jnp.float32)
    sig = jax.nn.sigmoid(gate_pre)
    gate_grad = hidden_grad * up_pre * (sig * (1.0 + gate_pre * (1.0 - sig)))
    up_grad = hidden_grad * (gate_pre * sig)
    both_grad = jnp.stack([gate_grad, up_grad], axis=1).astype(jnp.bfloat16).reshape(length, 2 * FF)
    gu_grad = jnp.dot(middle_bf.T, both_grad, preferred_element_type=jnp.float32).reshape(D, 2, FF)
    middle_grad = upstream + jnp.dot(both_grad, wgu.reshape(D, 2 * FF).T, preferred_element_type=jnp.float32)
    gain_attn = lax.optimization_barrier(jnp.sum(middle_grad * attn_n, axis=0))
    proj_grad = norm_back(middle_grad * gains[2], attn_n, attn_inv).astype(jnp.bfloat16)
    out_grad = jnp.dot(attn_bf.T, proj_grad, preferred_element_type=jnp.float32)
    mixed_grad = jnp.dot(proj_grad, wout.T, preferred_element_type=jnp.float32).astype(jnp.bfloat16)
    scores = causal_scores(query_bf, key_bf)
    probs = jnp.exp(scores - logsum)
    probs_bf = probs.astype(jnp.bfloat16)
    grad4 = mixed_grad.reshape(length, H, HD).astype(jnp.float32)
    value4 = value_bf.reshape(length, H, HD).astype(jnp.float32)
    prob_grad = jnp.einsum('qhd,khd->hqk', grad4, value4)
    delta = lax.optimization_barrier(jnp.sum((mixed_grad.astype(jnp.float32) * attn_bf.astype(jnp.float32)).reshape(length, H, HD), axis=-1)).T
    score_grad = (probs * (prob_grad - delta[..., None]) * HD ** (-0.5)).astype(jnp.bfloat16).astype(jnp.float32)
    key4 = key_bf.reshape(length, H, HD).astype(jnp.float32)
    query4 = query_bf.reshape(length, H, HD).astype(jnp.float32)
    query_grad = jnp.einsum('hqk,khd->qhd', score_grad, key4).reshape(length, D)
    key_grad = jnp.einsum('hqk,qhd->khd', score_grad, query4).reshape(length, D)
    value_grad = jnp.einsum('hqk,qhd->khd', probs_bf.astype(jnp.float32), grad4).reshape(length, D)
    gain_query = lax.optimization_barrier(jnp.sum(query_grad * query_n, axis=0))
    gain_key = lax.optimization_barrier(jnp.sum(key_grad * key_n, axis=0))
    query_raw = norm_back(query_grad * gains[0], query_n, query_inv)
    key_raw = norm_back(key_grad * gains[1], key_n, key_inv)
    qkv_grad = jnp.stack([query_raw, key_raw, value_grad], axis=1).astype(jnp.bfloat16).reshape(length, 3 * D)
    qkv_wgrad = jnp.dot(resid_bf.T, qkv_grad, preferred_element_type=jnp.float32).reshape(D, 3, D)
    resid_grad = middle_grad + jnp.dot(qkv_grad, wqkv.reshape(D, 3 * D).T, preferred_element_type=jnp.float32)
    gain_grad = jnp.stack([gain_query, gain_key, gain_attn, gain_mlp])
    return (resid_grad, (qkv_wgrad, out_grad, gu_grad, down_grad, gain_grad))

def reference(hidden_in, w_qkv, w_out, w_gate_up, w_down, norm_gains, grad_out):

    def one_sequence(totals, pair):
        seq_in, seq_grad = pair
        resid = seq_in.astype(jnp.float32)
        kept = []
        for layer in range(LAYERS):
            resid, saved = forward_layer(resid, w_qkv[layer], w_out[layer], w_gate_up[layer], w_down[layer], norm_gains[layer])
            kept.append(saved)
        result = resid.astype(jnp.bfloat16)
        upstream = seq_grad.astype(jnp.float32)
        grads = [None] * LAYERS
        for layer in reversed(range(LAYERS)):
            upstream, grads[layer] = backward_layer(upstream, w_qkv[layer], w_out[layer], w_gate_up[layer], w_down[layer], norm_gains[layer], kept[layer])
        stacked = tuple((jnp.stack([grads[layer][member] for layer in range(LAYERS)]) for member in range(5)))
        totals = tuple((older + newer for older, newer in zip(totals, stacked)))
        return (totals, (result, upstream))
    initial = (jnp.zeros(w_qkv.shape, jnp.float32), jnp.zeros(w_out.shape, jnp.float32), jnp.zeros(w_gate_up.shape, jnp.float32), jnp.zeros(w_down.shape, jnp.float32), jnp.zeros(norm_gains.shape, jnp.float32))
    totals, (outputs, grad_in) = lax.scan(one_sequence, initial, (hidden_in, grad_out))
    return (outputs, grad_in, totals[0], totals[1], totals[2], totals[3], totals[4])
```

```python
import functools

import jax
import jax.numpy as jnp
from jax import lax
from jax.experimental import pallas as pl
from jax.experimental.pallas import tpu as pltpu
from jax.sharding import PartitionSpec as P


D = 2048
HD = 128
LAYERS = 2


EPS = 1e-06
NEG = -1e30


def gather_cols(values):
    return lax.all_gather(values, "col", axis=1, tiled=True)


def col_sums(values):
    return lax.psum(values, "col")


def grad_cols(values):
    return lax.psum_scatter(
        values.astype(jnp.bfloat16), "col", scatter_dimension=1, tiled=True
    ).astype(jnp.float32)


def rms_shared(stacked):
    totals = col_sums(jnp.sum(stacked * stacked, axis=-1))
    inverse = lax.rsqrt(totals / D + EPS)[..., None]
    return (stacked * inverse, inverse)


def norm_back_shared(upstream, normed, inverse):
    center = col_sums(jnp.sum(upstream * normed, axis=-1)) / D
    return inverse * (upstream - normed * center[..., None])


def times_transposed(left, right):
    return lax.dot_general(
        left, right, (((1,), (1,)), ((), ())), preferred_element_type=jnp.float32
    )


def project(inputs_bf, weight):
    cols_full = gather_cols(inputs_bf)
    spread = lax.all_to_all(cols_full, "row", split_axis=1, concat_axis=0, tiled=True)
    return (
        lax.psum_scatter(
            jnp.dot(spread, weight, preferred_element_type=jnp.float32).astype(jnp.bfloat16),
            "row",
            scatter_dimension=0,
            tiled=True,
        ).astype(jnp.float32),
        spread,
    )


def project_back(grad_bf, weight, kept_input):
    piece = lax.all_gather(grad_bf, "row", axis=0, tiled=True)
    weight_grad = lax.dot_general(
        kept_input, piece, (((0,), (0,)), ((), ())), preferred_element_type=jnp.float32
    )
    input_grad = times_transposed(piece, weight)
    weight_grad, input_grad = (weight_grad, input_grad)
    returned = lax.all_to_all(
        input_grad.astype(jnp.bfloat16), "row", split_axis=0, concat_axis=1, tiled=True
    ).astype(input_grad.dtype)
    return (grad_cols(returned), weight_grad)


def scores_block(query_bf, key_full, heads):
    batch, local_len = (query_bf.shape[0], query_bf.shape[1])
    full_len = key_full.shape[1]
    query4 = query_bf.reshape(batch, local_len, heads, HD)
    key4 = key_full.reshape(batch, full_len, heads, HD)
    scores = jnp.einsum(
        "bqhd,bkhd->bhqk", query4, key4, preferred_element_type=jnp.float32
    ) * HD ** (-0.5)
    first = lax.axis_index("row") * local_len
    query_pos = first + lax.iota(jnp.int32, local_len)
    key_pos = lax.iota(jnp.int32, full_len)
    allowed = key_pos[None, :] <= query_pos[:, None]
    return jnp.where(allowed[None, None], scores, NEG)


def forward_layer(resid, w_qkv_blk, w_out_blk, w_gu_blk, w_down_blk, gains, batch):
    weights = (
        w_qkv_blk.reshape(w_qkv_blk.shape[0], -1),
        w_out_blk,
        w_gu_blk.reshape(w_gu_blk.shape[0], -1),
        w_down_blk,
    )
    tokens, width = resid.shape
    heads = width // HD
    local_len = tokens // batch
    proj, kept_resid = project(resid.astype(jnp.bfloat16), weights[0])
    proj = proj.reshape(tokens, 3, width)
    normed_qk, inverse_qk = rms_shared(jnp.stack([proj[:, 0], proj[:, 1]]))
    query_bf = (normed_qk[0] * gains[0]).astype(jnp.bfloat16)
    key_bf = (normed_qk[1] * gains[1]).astype(jnp.bfloat16)
    value_bf = proj[:, 2].astype(jnp.bfloat16)
    key_full, value_full = (
        lax.all_gather(key_bf.reshape(batch, local_len, width), "row", axis=1, tiled=True),
        lax.all_gather(value_bf.reshape(batch, local_len, width), "row", axis=1, tiled=True),
    )
    full_len = key_full.shape[1]
    scores = scores_block(query_bf.reshape(batch, local_len, width), key_full, heads)
    top = jnp.max(scores, axis=-1, keepdims=True)
    expo = jnp.exp(scores - top)
    total = jnp.sum(expo, axis=-1, keepdims=True)
    probs = expo / total
    logsum = top + jnp.log(total)
    attn = jnp.einsum(
        "bhqk,bkhd->bqhd",
        probs.astype(jnp.bfloat16),
        value_full.reshape(batch, full_len, heads, HD),
        preferred_element_type=jnp.float32,
    )
    attn_bf = attn.reshape(tokens, width).astype(jnp.bfloat16)
    attn_proj, kept_attn = project(attn_bf, weights[1])
    attn_normed, attn_inv = rms_shared(attn_proj[None])
    middle = resid + gains[2] * attn_normed[0]
    gate_up, kept_middle = project(middle.astype(jnp.bfloat16), weights[2])
    gate_up = gate_up.reshape(tokens, 2, -1)
    gate_pre, up_pre = (gate_up[:, 0], gate_up[:, 1])
    hidden_bf = (jax.nn.silu(gate_pre) * up_pre).astype(jnp.bfloat16)
    mlp_proj, kept_hidden = project(hidden_bf, weights[3])
    mlp_normed, mlp_inv = rms_shared(mlp_proj[None])
    output = middle + gains[3] * mlp_normed[0]
    saved = (
        weights,
        kept_resid,
        normed_qk,
        inverse_qk,
        query_bf,
        key_full,
        value_full,
        logsum,
        attn_bf,
        kept_attn,
        attn_normed,
        attn_inv,
        kept_middle,
        gate_pre,
        up_pre,
        kept_hidden,
        mlp_normed,
        mlp_inv,
    )
    return (output, saved)


def backward_layer(upstream, gains, saved, batch):
    weights = saved[0]
    (
        kept_resid,
        normed_qk,
        inverse_qk,
        query_bf,
        key_full,
        value_full,
        logsum,
        attn_bf,
        kept_attn,
        attn_normed,
        attn_inv,
        kept_middle,
        gate_pre,
        up_pre,
        kept_hidden,
        mlp_normed,
        mlp_inv,
    ) = saved[1:]
    tokens, width = upstream.shape
    heads = width // HD
    local_len = tokens // batch
    full_len = key_full.shape[1]
    gain_mlp = jnp.sum(upstream * mlp_normed[0], axis=0)
    mlp_grad = norm_back_shared((upstream * gains[3])[None], mlp_normed, mlp_inv)[0].astype(
        jnp.bfloat16
    )
    hidden_grad, down_grad = project_back(mlp_grad, weights[3], kept_hidden)
    sig = jax.nn.sigmoid(gate_pre)
    gate_grad = hidden_grad * up_pre * (sig * (1.0 + gate_pre * (1.0 - sig)))
    up_grad = hidden_grad * (gate_pre * sig)
    units = gate_pre.shape[1]
    both_grad = (
        jnp.stack([gate_grad, up_grad], axis=1).astype(jnp.bfloat16).reshape(tokens, 2 * units)
    )
    middle_back, gu_grad = project_back(both_grad, weights[2], kept_middle)
    gu_grad = gu_grad.reshape(-1, 2, units)
    middle_grad = upstream + middle_back
    gain_attn = jnp.sum(middle_grad * attn_normed[0], axis=0)
    proj_grad = norm_back_shared((middle_grad * gains[2])[None], attn_normed, attn_inv)[0].astype(
        jnp.bfloat16
    )
    mixed_back, out_grad = project_back(proj_grad, weights[1], kept_attn)
    mixed_grad = mixed_back.astype(jnp.bfloat16)
    scores = scores_block(query_bf.reshape(batch, local_len, width), key_full, heads)
    probs = jnp.exp(scores - logsum)
    probs_bf = probs.astype(jnp.bfloat16)
    grad4 = mixed_grad.reshape(batch, local_len, heads, HD)
    value4 = value_full.reshape(batch, full_len, heads, HD)
    prob_grad = jnp.einsum("bqhd,bkhd->bhqk", grad4, value4, preferred_element_type=jnp.float32)
    delta = jnp.sum(
        (mixed_grad.astype(jnp.float32) * attn_bf.astype(jnp.float32)).reshape(
            batch, local_len, heads, HD
        ),
        axis=-1,
    ).transpose(0, 2, 1)
    score_grad = (probs * (prob_grad - delta[..., None]) * HD ** (-0.5)).astype(jnp.bfloat16)
    query_grad = jnp.einsum(
        "bhqk,bkhd->bqhd",
        score_grad,
        key_full.reshape(batch, full_len, heads, HD),
        preferred_element_type=jnp.float32,
    ).reshape(tokens, width)
    key_part = jnp.einsum(
        "bhqk,bqhd->bkhd",
        score_grad,
        query_bf.reshape(batch, local_len, heads, HD),
        preferred_element_type=jnp.float32,
    )
    value_part = jnp.einsum("bhqk,bqhd->bkhd", probs_bf, grad4, preferred_element_type=jnp.float32)
    key_grad, value_grad = (
        lax.psum_scatter(
            key_part.astype(jnp.bfloat16), "row", scatter_dimension=1, tiled=True
        ).astype(jnp.float32),
        lax.psum_scatter(
            value_part.astype(jnp.bfloat16), "row", scatter_dimension=1, tiled=True
        ).astype(jnp.float32),
    )
    stacked = jnp.stack([query_grad, key_grad.reshape(tokens, width)])
    gain_qk = jnp.sum(stacked * normed_qk, axis=1)
    raw_qk = norm_back_shared(stacked * gains[0:2][:, None, :], normed_qk, inverse_qk)
    qkv_grad = jnp.stack([raw_qk[0], raw_qk[1], value_grad.reshape(tokens, width)], axis=1)
    qkv_grad = qkv_grad.astype(jnp.bfloat16).reshape(tokens, 3 * width)
    qkv_back, qkv_wgrad = project_back(qkv_grad, weights[0], kept_resid)
    qkv_wgrad = qkv_wgrad.reshape(-1, 3, width)
    resid_grad = middle_grad + qkv_back
    gain_grad = jnp.stack([gain_qk[0], gain_qk[1], gain_attn, gain_mlp])
    return (resid_grad, (qkv_wgrad, out_grad, gu_grad, down_grad), gain_grad)


def plain_body(hidden_in, w_qkv, w_out, w_gate_up, w_down, norm_gains, grad_out):
    batch, local_len, width = hidden_in.shape
    resid = hidden_in.reshape(batch * local_len, width).astype(jnp.float32)
    kept = []
    for layer in range(LAYERS):
        resid, saved = forward_layer(
            resid,
            w_qkv[layer],
            w_out[layer],
            w_gate_up[layer],
            w_down[layer],
            norm_gains[layer],
            batch,
        )
        kept.append(saved)
    hidden_out = resid.astype(jnp.bfloat16).reshape(batch, local_len, width)
    upstream = grad_out.reshape(batch * local_len, width).astype(jnp.float32)
    collected = [None] * LAYERS
    gain_parts = [None] * LAYERS
    for layer in reversed(range(LAYERS)):
        upstream, grads, gain_grad = backward_layer(upstream, norm_gains[layer], kept[layer], batch)
        collected[layer] = grads
        gain_parts[layer] = gain_grad
    stacks = [
        jnp.stack([collected[layer][member] for layer in range(LAYERS)]) for member in range(4)
    ]
    stacks = (
        lax.psum(stacks[0].astype(jnp.bfloat16), "dp").astype(jnp.float32),
        lax.psum(stacks[1].astype(jnp.bfloat16), "dp").astype(jnp.float32),
        lax.psum(stacks[2].astype(jnp.bfloat16), "dp").astype(jnp.float32),
        lax.psum(stacks[3].astype(jnp.bfloat16), "dp").astype(jnp.float32),
    )
    gain_total = lax.psum(jnp.stack(gain_parts), ("dp", "row"))
    grad_in = upstream.reshape(batch, local_len, width)
    return (hidden_out, grad_in, stacks[0], stacks[1], stacks[2], stacks[3], gain_total)


BF = jnp.bfloat16
F32 = jnp.float32


def fits_plane(mesh):
    sizes = dict(mesh.shape)
    return sizes["dp"] == 4 and sizes["row"] == 2 and sizes["col"] == 4


def cat(*parts):
    return jnp.concatenate(parts, axis=0)


def add_bf(left, right):
    return (left.astype(F32) + right.astype(F32)).astype(BF)


def swap_core(values):
    return lax.ppermute(values, "col", [(j, j ^ 1) for j in range(4)])


def swap_x(values):
    return lax.ppermute(values, "col", [(j, j ^ 2) for j in range(4)])


def swap_y(values):
    return lax.ppermute(values, "row", [(0, 1), (1, 0)])


HOPS = ((swap_y, swap_x), (swap_x, swap_y))


def gather_tokens(block, stream):
    near, far = HOPS[stream % 2]
    pair = cat(block, near(block))
    quad = cat(pair, far(pair))
    return cat(quad, swap_core(quad))


def scatter_tokens(partial, stream):
    near, far = HOPS[stream % 2]
    half = partial.shape[0] // 2
    quad = add_bf(partial[:half], swap_core(partial[half:]))
    half //= 2
    pair = add_bf(quad[:half], far(quad[half:]))
    half //= 2
    return pair[:half].astype(F32) + near(pair[half:]).astype(F32)


def token_positions(stream, block):
    row = lax.axis_index("row")
    col = lax.axis_index("col")
    core, chip = (col % 2, col // 2)
    near, far = (row, chip) if stream % 2 == 0 else (chip, row)
    index = jnp.arange(8)
    far_bit = (index // 2) % 2
    near_bit = index % 2
    core_at = core ^ (index // 4)
    far_at = far ^ far_bit
    near_at = near ^ near_bit
    row_at, chip_at = (near_at, far_at) if stream % 2 == 0 else (far_at, near_at)
    first = (row_at * 4 + chip_at * 2 + core_at) * block
    return (first[:, None] + jnp.arange(block)[None, :]).reshape(-1)


def plane_sum(stats, stream):
    near, far = HOPS[stream % 2]
    kinds, tokens = stats.shape
    view = stats.reshape(kinds, 2, 2, 2, tokens // 8)
    view = view + jnp.flip(swap_core(view), 1)
    view = view + jnp.flip(far(view), 2)
    view = view + jnp.flip(near(view), 3)
    return view.reshape(kinds, tokens)


def exchange(blocks_of, flip_a, flip_b, back):
    pairs = []
    for row in range(2):
        for chip in range(2):
            for core in range(2):
                source = row * 4 + chip * 2 + core
                target = (chip ^ flip_a) * 4 + row * 2 + (core ^ flip_b)
                pairs.append((target, source) if back else (source, target))
    return lax.ppermute(blocks_of, ("row", "col"), pairs)


def place():
    row = lax.axis_index("row")
    col = lax.axis_index("col")
    return (row, col // 2, col % 2)


FLIPS = ((0, 0), (0, 1), (1, 0), (1, 1))


def columns_weight(blk):
    row = lax.axis_index("row")
    rows, parts, cols = blk.shape
    half = cols // 2
    kept = lax.dynamic_slice_in_dim(blk, row * half, half, 2).reshape(rows, parts * half)
    sent = lax.dynamic_slice_in_dim(blk, (1 - row) * half, half, 2).reshape(rows, parts * half)
    got = swap_y(sent)
    full = jnp.zeros((2 * rows, parts * half), blk.dtype)
    full = lax.dynamic_update_slice_in_dim(full, kept, row * rows, 0)
    return lax.dynamic_update_slice_in_dim(full, got, (1 - row) * rows, 0)


def columns_grad(grad, parts):
    row = lax.axis_index("row")
    rows = grad.shape[0] // 2
    half = grad.shape[1] // parts
    kept = lax.dynamic_slice_in_dim(grad, row * rows, rows, 0)
    got = swap_y(lax.dynamic_slice_in_dim(grad, (1 - row) * rows, rows, 0))
    low = jnp.where(row == 0, kept, got).reshape(rows, parts, 1, half)
    high = jnp.where(row == 0, got, kept).reshape(rows, parts, 1, half)
    return jnp.concatenate([low, high], axis=2).reshape(rows, parts * 2 * half)


def rows_weight(blk):
    row, chip, core = place()
    rows, cols = blk.shape
    part = rows // 4
    view = blk.reshape(2, 2, part, cols)
    full = jnp.zeros((part, 4 * cols), blk.dtype)
    for flip_a, flip_b in FLIPS:
        sent = lax.dynamic_slice(
            view, (core ^ flip_b, chip ^ flip_a, 0, 0), (1, 1, part, cols)
        ).reshape(part, cols)
        got = exchange(sent, flip_a, flip_b, False)
        quarter = 2 * (row ^ flip_a) + (core ^ flip_b)
        full = lax.dynamic_update_slice_in_dim(full, got, quarter * cols, 1)
    return full


def rows_grad(grad):
    row, chip, core = place()
    part, width = grad.shape
    cols = width // 4
    full = jnp.zeros((4 * part, cols), grad.dtype)
    for flip_a, flip_b in FLIPS:
        quarter = 2 * (row ^ flip_a) + (core ^ flip_b)
        got = exchange(
            lax.dynamic_slice_in_dim(grad, quarter * cols, cols, 1), flip_a, flip_b, True
        )
        slot = 2 * (core ^ flip_b) + (chip ^ flip_a)
        full = lax.dynamic_update_slice_in_dim(full, got, slot * part, 0)
    return full


def hop_z(values, pairs):
    return lax.ppermute(values, "dp", pairs)


def sum_planes(chunk):
    plane = lax.axis_index("dp")
    half = chunk.shape[0] // 2
    low = plane < 2
    part = add_bf(chunk, hop_z(chunk, [(0, 1), (3, 2)]))
    kept = lax.dynamic_slice_in_dim(part, jnp.where(low, 0, half), half, 0)
    sent = lax.dynamic_slice_in_dim(part, jnp.where(low, half, 0), half, 0)
    done = add_bf(kept, hop_z(sent, [(1, 2), (2, 1)]))
    other = hop_z(done, [(1, 2), (2, 1)])
    total = jnp.where(low, cat(done, other), cat(other, done))
    outer = hop_z(total, [(1, 0), (2, 3)])
    return jnp.where((plane == 1) | (plane == 2), total, outer)


def attend_kernel(pos_q, pos_k, inv_q, inv_k, gain_q, gain_k, q, k, v, out):
    query = (q[...].astype(F32) * inv_q[...] * gain_q[...]).astype(BF)
    key = (k[...].astype(F32) * inv_k[...] * gain_k[...]).astype(BF)
    scores = times_transposed(query, key) * HD ** (-0.5)
    scores = jnp.where(pos_k[...] <= pos_q[...], scores, NEG)
    expo = jnp.exp(scores - jnp.max(scores, axis=-1, keepdims=True))
    probs = (expo / jnp.sum(expo, axis=-1, keepdims=True)).astype(BF)
    out[...] = jnp.dot(probs, v[...], preferred_element_type=F32).astype(BF)


def head_specs(tokens, heads):
    def whole(shape):
        return pl.BlockSpec(shape, lambda h: (0, 0))

    def cols(first):
        return pl.BlockSpec((tokens, HD), lambda h: (0, first + h))

    gain = pl.BlockSpec((1, HD), lambda h: (0, h))
    common = [whole((tokens, 1)), whole((1, tokens)), whole((tokens, 1)), whole((tokens, 1)), gain, gain]
    return common + [cols(0), cols(heads), cols(2 * heads)], cols(0), gain


def attend(pos, inverse, gain_q, gain_k, qkv):
    tokens = qkv.shape[0]
    heads = gain_q.shape[0] // HD
    specs, cols, _ = head_specs(tokens, heads)
    return pl.pallas_call(
        attend_kernel,
        grid=(heads,),
        in_specs=specs,
        out_specs=cols,
        out_shape=jax.ShapeDtypeStruct((tokens, heads * HD), BF),
        cost_estimate=pl.CostEstimate(
            flops=4 * heads * tokens * tokens * HD,
            bytes_accessed=8 * tokens * heads * HD,
            transcendentals=heads * tokens * tokens,
        ),
    )(
        pos[:, None], pos[None, :], inverse[0][:, None], inverse[1][:, None],
        gain_q[None, :], gain_k[None, :], qkv, qkv, qkv,
    )


def attend_back_kernel(
    pos_q, pos_k, inv_q, inv_k, gain_q, gain_k, q, k, v, o, do,
    dq_out, dk_out, dv_out, stat_q, stat_k, dgain_q, dgain_k,
):
    scale = HD ** (-0.5)
    normed_q = q[...].astype(F32) * inv_q[...]
    normed_k = k[...].astype(F32) * inv_k[...]
    query = (normed_q * gain_q[...]).astype(BF)
    key = (normed_k * gain_k[...]).astype(BF)
    scores = times_transposed(query, key) * scale
    scores = jnp.where(pos_k[...] <= pos_q[...], scores, NEG)
    expo = jnp.exp(scores - jnp.max(scores, axis=-1, keepdims=True))
    probs = expo / jnp.sum(expo, axis=-1, keepdims=True)
    grad = do[...]
    delta = jnp.sum(grad.astype(F32) * o[...].astype(F32), axis=-1, keepdims=True)
    score_grad = (probs * (times_transposed(grad, v[...]) - delta) * scale).astype(BF)
    over_rows = (((0,), (0,)), ((), ()))
    dv_out[...] = lax.dot_general(
        probs.astype(BF), grad, over_rows, preferred_element_type=F32
    ).astype(BF)
    dq = jnp.dot(score_grad, key, preferred_element_type=F32)
    dk = lax.dot_general(score_grad, query, over_rows, preferred_element_type=F32)
    dgain_q[...] = jnp.sum(dq * normed_q, axis=0, keepdims=True)
    dgain_k[...] = jnp.sum(dk * normed_k, axis=0, keepdims=True)
    dq = dq * gain_q[...]
    dk = dk * gain_k[...]
    stat_q[0] = jnp.sum(dq * normed_q, axis=-1, keepdims=True)
    stat_k[0] = jnp.sum(dk * normed_k, axis=-1, keepdims=True)
    dq_out[...] = dq
    dk_out[...] = dk


def attend_back(pos, inverse, gain_q, gain_k, qkv, out, grad):
    tokens = qkv.shape[0]
    width = gain_q.shape[0]
    heads = width // HD
    specs, cols, gain = head_specs(tokens, heads)
    stat = pl.BlockSpec((1, tokens, 1), lambda h: (h, 0, 0))
    return pl.pallas_call(
        attend_back_kernel,
        grid=(heads,),
        in_specs=specs + [cols, cols],
        out_specs=[cols, cols, cols, stat, stat, gain, gain],
        out_shape=[
            jax.ShapeDtypeStruct((tokens, width), F32),
            jax.ShapeDtypeStruct((tokens, width), F32),
            jax.ShapeDtypeStruct((tokens, width), BF),
            jax.ShapeDtypeStruct((heads, tokens, 1), F32),
            jax.ShapeDtypeStruct((heads, tokens, 1), F32),
            jax.ShapeDtypeStruct((1, width), F32),
            jax.ShapeDtypeStruct((1, width), F32),
        ],
        cost_estimate=pl.CostEstimate(
            flops=10 * heads * tokens * tokens * HD,
            bytes_accessed=20 * tokens * heads * HD,
            transcendentals=heads * tokens * tokens,
        ),
    )(
        pos[:, None], pos[None, :], inverse[0][:, None], inverse[1][:, None],
        gain_q[None, :], gain_k[None, :], qkv, qkv, qkv, out, grad,
    )


def dot_bf(left, right):
    return jnp.dot(left, right, preferred_element_type=F32).astype(BF)


def over_tokens(lefts, rights):
    return lax.dot_general(
        cat(*lefts), cat(*rights), (((0,), (0,)), ((), ())), preferred_element_type=F32
    ).astype(BF)


def own_rms(values):
    inverse = lax.rsqrt(jnp.mean(values * values, axis=-1, keepdims=True) + EPS)
    return (values * inverse, inverse)


def own_norm_back(upstream, normed, inverse):
    center = jnp.mean(upstream * normed, axis=-1, keepdims=True)
    return inverse * (upstream - normed * center)


def plane_forward(resid, weights, gains, positions):
    w_qkv, w_out, w_gu, w_down = weights
    gain_q, gain_k, gain_attn, gain_mlp = gains
    streams = range(len(resid))
    units = w_down.shape[0]
    width = w_out.shape[0]
    saved = []
    output = []
    for s in streams:
        full_in = gather_tokens(resid[s].astype(BF), s)
        qkv = dot_bf(full_in, w_qkv)
        wide = qkv.astype(F32)
        squares = jnp.stack(
            [jnp.sum(wide[:, :width] ** 2, axis=-1), jnp.sum(wide[:, width : 2 * width] ** 2, axis=-1)]
        )
        inverse = lax.rsqrt(plane_sum(squares, s) / resid[s].shape[1] + EPS)
        mixed = attend(positions[s], inverse, gain_q, gain_k, qkv)
        attn_normed, attn_inv = own_rms(scatter_tokens(dot_bf(mixed, w_out), s))
        middle = resid[s] + gain_attn * attn_normed
        full_mid = gather_tokens(middle.astype(BF), s)
        gate_up = dot_bf(full_mid, w_gu)
        wide = gate_up.astype(F32)
        hidden = (jax.nn.silu(wide[:, :units]) * wide[:, units:]).astype(BF)
        mlp_normed, mlp_inv = own_rms(scatter_tokens(dot_bf(hidden, w_down), s))
        output.append(middle + gain_mlp * mlp_normed)
        saved.append(
            (full_in, qkv, inverse, mixed, attn_normed, attn_inv, full_mid, gate_up, hidden, mlp_normed, mlp_inv)
        )
    return output, saved


def plane_backward(upstream, weights, gains, positions, saved, last):
    w_qkv, w_out, w_gu, w_down = weights
    gain_q, gain_k, gain_attn, gain_mlp = gains
    streams = range(len(upstream))
    units = w_down.shape[0]
    full_dim = w_out.shape[1]
    hid, d_mlp, mid, d_gu, mix, d_attn, inp, d_qkv = ([] for _ in range(8))
    g_q = g_k = g_attn = g_mlp = 0.0
    result = []
    for s in streams:
        (full_in, qkv, inverse, mixed, attn_normed, attn_inv, full_mid, gate_up, hidden, mlp_normed, mlp_inv) = saved[s]
        dz = upstream[s]
        g_mlp += jnp.sum(dz * mlp_normed, axis=0)
        dm = gather_tokens(own_norm_back(dz * gain_mlp, mlp_normed, mlp_inv).astype(BF), s)
        hid.append(hidden)
        d_mlp.append(dm)
        dh = times_transposed(dm, w_down).astype(BF).astype(F32)
        gate = gate_up[:, :units].astype(F32)
        up = gate_up[:, units:].astype(F32)
        sig = jax.nn.sigmoid(gate)
        dgu = jnp.concatenate(
            [dh * up * (sig * (1.0 + gate * (1.0 - sig))), dh * (gate * sig)], axis=1
        ).astype(BF)
        mid.append(full_mid)
        d_gu.append(dgu)
        dy = dz + scatter_tokens(times_transposed(dgu, w_gu).astype(BF), s)
        g_attn += jnp.sum(dy * attn_normed, axis=0)
        da = gather_tokens(own_norm_back(dy * gain_attn, attn_normed, attn_inv).astype(BF), s)
        mix.append(mixed)
        d_attn.append(da)
        dmix = times_transposed(da, w_out).astype(BF)
        dq, dk, dv, stat_q, stat_k, dgq, dgk = attend_back(
            positions[s], inverse, gain_q, gain_k, qkv, mixed, dmix
        )
        g_q += dgq[0]
        g_k += dgk[0]
        stats = jnp.stack([jnp.sum(stat_q, axis=0)[:, 0], jnp.sum(stat_k, axis=0)[:, 0]])
        center = plane_sum(stats, s) / full_dim
        width = dq.shape[1]
        inv_q, inv_k = (inverse[0][:, None], inverse[1][:, None])
        raw = qkv.astype(F32)
        dqkv = jnp.concatenate(
            [
                (inv_q * (dq - raw[:, :width] * inv_q * center[0][:, None])).astype(BF),
                (inv_k * (dk - raw[:, width : 2 * width] * inv_k * center[1][:, None])).astype(BF),
                dv,
            ],
            axis=1,
        )
        inp.append(full_in)
        d_qkv.append(dqkv)
        result.append(dy + scatter_tokens(times_transposed(dqkv, w_qkv).astype(BF), s))
    down = sum_planes(rows_grad(over_tokens(hid, d_mlp)))
    gu = sum_planes(columns_grad(over_tokens(mid, d_gu), 2))
    out = sum_planes(rows_grad(over_tokens(mix, d_attn)))
    qkv = sum_planes(columns_grad(over_tokens(inp, d_qkv), 3))
    return result, (qkv, out, gu, down), (g_q, g_k, g_attn, g_mlp)


def to_tokens(values):
    moved = lax.all_to_all(values, "col", split_axis=1, concat_axis=2, tiled=True)
    return [moved[s] for s in range(moved.shape[0])]


def from_tokens(streams):
    return lax.all_to_all(jnp.stack(streams), "col", split_axis=2, concat_axis=1, tiled=True)


def plane_body(hidden_in, w_qkv, w_out, w_gate_up, w_down, norm_gains, grad_out):
    row = lax.axis_index("row")
    layers = w_qkv.shape[0]
    resid = [values.astype(F32) for values in to_tokens(hidden_in)]
    upstream = [values.astype(F32) for values in to_tokens(grad_out)]
    positions = [token_positions(s, resid[s].shape[0]) for s in range(len(resid))]
    wide_gains = lax.all_gather(norm_gains[:, 2:], "col", axis=2, tiled=True)
    share = norm_gains.shape[2] // 2
    own_gains = lax.dynamic_slice_in_dim(norm_gains[:, :2], row * share, share, 2)
    weights, gains, kept = [], [], []
    for layer in range(layers):
        weights.append(
            (
                columns_weight(w_qkv[layer]),
                rows_weight(w_out[layer]),
                columns_weight(w_gate_up[layer]),
                rows_weight(w_down[layer]),
            )
        )
        gains.append(
            (own_gains[layer, 0], own_gains[layer, 1], wide_gains[layer, 0], wide_gains[layer, 1])
        )
    for layer in range(layers):
        resid, saved = plane_forward(resid, weights[layer], gains[layer], positions)
        kept.append(saved)
    hidden_out = from_tokens([values.astype(BF) for values in resid])
    grads, narrow, wide = ([None] * layers for _ in range(3))
    for layer in reversed(range(layers)):
        upstream, grads[layer], gain_parts = plane_backward(
            upstream, weights[layer], gains[layer], positions, kept[layer], layer == 0
        )
        narrow[layer] = jnp.stack(gain_parts[:2])
        wide[layer] = jnp.stack(gain_parts[2:])
    grad_in = from_tokens(upstream)
    shapes = (w_qkv.shape, w_out.shape, w_gate_up.shape, w_down.shape)
    outs = [
        jnp.stack([grads[layer][member] for layer in range(layers)]).astype(F32).reshape(shapes[member])
        for member in range(4)
    ]
    spread = jnp.zeros(norm_gains[:, :2].shape, F32)
    spread = lax.dynamic_update_slice_in_dim(spread, jnp.stack(narrow), row * share, 2)
    narrow_total = lax.psum(spread, ("dp", "row"))
    wide_total = lax.psum(jnp.stack(wide), ("dp", "row", "col"))
    col = lax.axis_index("col")
    wide_total = lax.dynamic_slice_in_dim(wide_total, col * 2 * share, 2 * share, 2)
    gain_total = jnp.concatenate([narrow_total, wide_total], axis=1)
    return (hidden_out, grad_in, outs[0], outs[1], outs[2], outs[3], gain_total)


def solution(mesh):
    return jax.shard_map(
        plane_body if fits_plane(mesh) else plain_body,
        mesh=mesh,
        in_specs=(
            P("dp", "row", "col"),
            P(None, "row", None, "col"),
            P(None, "row", "col"),
            P(None, "row", None, "col"),
            P(None, "row", "col"),
            P(None, None, "col"),
            P("dp", "row", "col"),
        ),
        out_specs=(
            P("dp", "row", "col"),
            P("dp", "row", "col"),
            P(None, "row", None, "col"),
            P(None, "row", "col"),
            P(None, "row", None, "col"),
            P(None, "row", "col"),
            P(None, None, "col"),
        ),
        check_vma=False,
    )
```
